32 devices in a mesh: expert: 8 (over z, x), replica: 2 (over y), section: 2 (over core).
Axes of the slice: x: 2, y: 2, z: 4, core: 2. Of those that a mesh axis runs over, the one named last changes fastest.
Arguments:
- frames: bfloat16 [2, 2048, 1024], P('section', ('expert', 'replica')), may hold values from -6 to 6
- cotangent: bfloat16 [2, 2048, 1024], P('section', ('expert', 'replica')), may hold values from -3 to 3
- expert_ids: int32 [2, 2048, 8], P('section', ('expert', 'replica')), may hold values from 0 to 15, all different within a row; in each aligned block of 128 rows (0 to 127, 128 to 255, ..., all dimensions but the last counted through in order) at most 64 rows name the same one
- gate_weights: float32 [2, 2048, 8], P('section', ('expert', 'replica')), may hold values from 0.05 to 1
- weight_in: bfloat16 [2, 16, 1024, 768], P('section', 'expert', 'replica'), may hold values from -0.1875 to 0.1875
- weight_out: bfloat16 [2, 16, 768, 1024], P('section', 'expert', None, 'replica'), may hold values from -0.21875 to 0.21875
Outputs:
- sent_grads: bfloat16 [2, 2048, 1024], P('section', ('expert', 'replica'))
- grad_in: bfloat16 [2, 16, 1024, 768], P('section', 'expert', 'replica')
- grad_out: bfloat16 [2, 16, 768, 1024], P('section', 'expert', None, 'replica')
The draws below stay inside these ranges and needn't reach their ends.
Inputs may be any that keep to these rules, and one draw needn't show every extreme that they name: `expert_ids`: each row names 8 different experts; among the rows of one device no expert is named more than 64 times, a bound that some block reaches.
All inputs are finite; a program needn't handle non-finite values.
Results may differ from the reference program's by a relative error of at most 0.012.
Values may be sent and summed in bfloat16 or wider, within the bound.
No kernel may reach another device: no remote copies, remote signals or barrier semaphores. Data moves between devices by JAX's collectives and lax.ppermute only.
A program may use at most 64 MiB of HBM per device.

```python
import math
import jax
import jax.numpy as jnp
import numpy as np
from jax import lax

D = 1024
H = 768
TOPK = 8
TOK_DEV = 128
EXPERTS = 16
MOST = 64
TOKENS = 2048
N_EXPERT = 8
N_REPLICA = 2


def shard_levels(own_key, extent, split, smallest, high):
    factor_of, own = 1.0, jax.random.fold_in(own_key, 6)
    for axis_at, parts in split:
        steps = jnp.exp(jax.random.uniform(jax.random.fold_in(own, axis_at), (parts,), jnp.float32, smallest / len(split), high / len(split)))
        factor_of = factor_of * jnp.repeat(steps, extent[axis_at] // parts).reshape([-1 if axis == axis_at else 1 for axis in range(len(extent))])
    return factor_of


def assign_block(own_key, own, number, rows, amount, top, limit, skew):
    sequence = jax.random.permutation(own_key, amount)
    packed, common = shares(amount, rows * top, limit, skew, True), shares(amount, rows * top, limit, skew, False)
    places = jnp.arange(amount)

    def named(lengths, rotation):
        used = int((lengths > 0).sum())
        fixed = max(1, used // 4)
        moved = fixed + (places - fixed + rotation * (used - fixed)) % max(1, amount - fixed)
        return jnp.zeros((amount,), jnp.int32).at[sequence[jnp.where(places < fixed, places, moved)]].set(jnp.asarray(lengths, jnp.int32))

    lengths = jnp.where(number % 4 == 0, named(packed, number // 4), named(common, number - number // 4 - 1))
    mixed = jax.random.permutation(jax.random.fold_in(own, 3), amount)
    giver, taker = mixed[0:amount // 2 * 2:2], mixed[1:amount // 2 * 2:2]
    room = jnp.minimum(lengths[giver] - 1, limit - lengths[taker]) // 2
    room = jnp.where((giver == sequence[0]) | (taker == sequence[0]) | (lengths[taker] == 0), 0, jnp.maximum(room, 0))
    moved = jax.random.randint(jax.random.fold_in(own, 4), (amount // 2,), 0, 1 << 20) % (room + 1)
    lengths = lengths.at[giver].add(-moved).at[taker].add(moved)
    members = jnp.searchsorted(jnp.cumsum(lengths), jnp.arange(rows * top), side="right").astype(jnp.int32)
    grid = members.reshape(top, rows).T
    grid = grid[jax.random.permutation(jax.random.fold_in(own, 1), rows)]
    rotation = jax.random.randint(jax.random.fold_in(own, 2), (rows, 1), 0, top)
    return jnp.take_along_axis(grid, (jnp.arange(top)[None, :] + rotation) % top, axis=1)


def shares(amount, total, bound, slope, full):
    loads = [(1 << 20) // math.isqrt(grade ** slope) + 1 for grade in range(1, amount + 1)]
    largest = bound if full else min(bound, max(-(-total // amount), total * loads[0] // sum(loads)))
    least = 1 if total - largest >= amount - 1 else 0
    counts, spare = [largest] + [least] * (amount - 1), total - largest - least * (amount - 1)
    while spare > 0:
        candidates = [i for i in range(1, amount) if counts[i] < largest] or [i for i in range(1, amount) if counts[i] < bound]
        mass, left = sum([loads[i] for i in candidates]), spare
        for i in candidates:
            more = min(bound - counts[i], max(1, left * loads[i] // mass), spare)
            counts[i] = counts[i] + more
            spare = spare - more
    return np.array(counts)


def noise(stream_key, dims, deviation, bound, split=(), held_as=jnp.bfloat16):
    level = shard_levels(stream_key, dims, split, -0.22, 0.18) if split else 1.0
    array = jax.random.normal(stream_key, dims, jnp.float32) * deviation * level
    return jnp.minimum(jnp.maximum(array, -bound), bound).astype(held_as)


def setup_inputs(seed: int = 0) -> dict:
    seeds = jax.random.split(jax.random.key(seed), 7)
    frames = noise(seeds[0], (2, TOKENS, D), 1.0, 6.0, ((0, 2), (1, 16)))
    cotangent = noise(seeds[1], (2, TOKENS, D), 0.5, 3.0, ((0, 2), (1, 16)))
    expert_ids_keys = jax.random.split(jax.random.fold_in(seeds[2], 1), 2 * TOKENS // TOK_DEV)
    expert_ids_turns = jax.random.permutation(jax.random.fold_in(seeds[2], 3), 2 * TOKENS // TOK_DEV)
    expert_ids = jax.vmap(lambda own, number: assign_block(jax.random.fold_in(seeds[2], 2), own, number, TOK_DEV, EXPERTS, TOPK, MOST, 2))(expert_ids_keys, expert_ids_turns).reshape((2, TOKENS, TOPK))
    gate_weights = jnp.clip(jnp.exp(math.log(1.0) - 2.9957323 * jax.random.uniform(seeds[3], (2, TOKENS, TOPK), jnp.float32) ** shard_levels(seeds[3], (2, TOKENS, TOPK), ((0, 2), (1, 16)), -0.2, 0.2)), 0.05, 1.0)
    weight_in = noise(seeds[4], (2, EXPERTS, D, H), D ** -0.5, 0.1875, ((0, 2), (1, 8), (2, 2)))
    weight_out = noise(seeds[5], (2, EXPERTS, H, D), H ** -0.5, 0.21875, ((0, 2), (1, 8), (3, 2)))
    return dict(frames=frames, cotangent=cotangent, expert_ids=expert_ids, gate_weights=gate_weights, weight_in=weight_in, weight_out=weight_out)


def silu_slope(value):
    sigma = jax.nn.sigmoid(value)
    return sigma * (1.0 + value * (1.0 - sigma))


def one_layer(frames, cotangent, expert_ids, gate_weights, weight_in, weight_out):
    groups = N_EXPERT * N_REPLICA
    per_group = TOK_DEV * TOPK
    ids = expert_ids.reshape(groups, per_group)
    onehot = (ids[:, :, None] == jnp.arange(EXPERTS, dtype=jnp.int32)[None, None, :]).astype(jnp.int32)
    position = jnp.sum((jnp.cumsum(onehot, 1) - 1) * onehot, 2).astype(jnp.int32)
    group_index = jnp.arange(groups, dtype=jnp.int32)[:, None]
    column = group_index * MOST + position
    row_flat = group_index * per_group + jnp.arange(per_group, dtype=jnp.int32)[None, :]
    table = jnp.full((EXPERTS, groups * MOST), TOKENS * TOPK, jnp.int32).at[ids, column].set(row_flat)
    padded_x = jnp.concatenate([frames, jnp.zeros((1, D), jnp.bfloat16)], 0)
    padded_g = jnp.concatenate([cotangent, jnp.zeros((1, D), jnp.bfloat16)], 0)
    gate_flat = jnp.concatenate([gate_weights.reshape(-1), jnp.zeros((1,), jnp.float32)], 0)

    def one_expert(carry, inputs):
        rows, w_first, w_second = inputs
        token_rows = rows // TOPK
        inputs_x = padded_x[token_rows]
        slot_grad = (gate_flat[rows][:, None] * padded_g[token_rows].astype(jnp.float32)).astype(jnp.bfloat16)
        pre = jnp.dot(inputs_x, w_first, preferred_element_type=jnp.float32)
        hidden = jax.nn.silu(pre).astype(jnp.bfloat16)
        hidden_grad = jnp.dot(slot_grad, w_second.T, preferred_element_type=jnp.float32)
        pre_grad = (hidden_grad * silu_slope(pre)).astype(jnp.bfloat16)
        row_grad = jnp.dot(pre_grad, w_first.T, preferred_element_type=jnp.float32).astype(jnp.bfloat16)
        carry = carry.at[token_rows].add(row_grad.astype(jnp.float32))
        shaped_x = inputs_x.astype(jnp.float32).reshape(N_EXPERT, N_REPLICA, MOST, D)
        shaped_g = slot_grad.astype(jnp.float32).reshape(N_EXPERT, N_REPLICA, MOST, D)
        shaped_h = hidden.astype(jnp.float32).reshape(N_EXPERT, N_REPLICA, MOST, H)
        shaped_p = pre_grad.astype(jnp.float32).reshape(N_EXPERT, N_REPLICA, MOST, H)
        part_in = jnp.einsum("irmd,irmh->rdh", shaped_x, shaped_p).astype(jnp.bfloat16)
        part_out = jnp.einsum("irmh,irmd->rhd", shaped_h, shaped_g).astype(jnp.bfloat16)
        total_in = jnp.sum(part_in.astype(jnp.float32), 0).astype(jnp.bfloat16)
        total_out = jnp.sum(part_out.astype(jnp.float32), 0).astype(jnp.bfloat16)
        return carry, (total_in, total_out)

    start = jnp.zeros((TOKENS + 1, D), jnp.float32)
    summed, grads = lax.scan(one_expert, start, (table, weight_in, weight_out))
    return summed[:TOKENS].astype(jnp.bfloat16), grads[0], grads[1]


def reference(frames, cotangent, expert_ids, gate_weights, weight_in, weight_out):
    lower = one_layer(frames[0], cotangent[0], expert_ids[0], gate_weights[0], weight_in[0], weight_out[0])
    upper = one_layer(frames[1], cotangent[1], expert_ids[1], gate_weights[1], weight_in[1], weight_out[1])
    sent_grads = jnp.stack([upper[0], lower[0]], 0)
    grad_in = jnp.stack([lower[1], upper[1]], 0)
    grad_out = jnp.stack([lower[2], upper[2]], 0)
    return sent_grads, grad_in, grad_out
```

```python
import jax
import jax.numpy as jnp
from jax import lax
from jax.sharding import PartitionSpec as P


F32 = jnp.float32
BF16 = jnp.bfloat16


def grid_of(count):
    inner = 1
    while inner * inner * 4 <= count and count % (inner * 2) == 0:
        inner *= 2
    return count // inner, inner


def ring_shift(value, distance, outer, inner, along_outer):
    route = []
    for i in range(outer * inner):
        z, x = divmod(i, inner)
        if along_outer:
            route.append((i, (z + distance) % outer * inner + x))
        else:
            route.append((i, z * inner + (x + distance) % inner))
    return lax.ppermute(value, "expert", route)


def gather_blocks(own, outer, inner):
    slots = []
    column = own
    for dz in range(outer):
        if dz:
            column = ring_shift(column, 1, outer, inner, True)
        row = [column]
        for _ in range(inner - 1):
            row.append(ring_shift(row[-1], 1, outer, inner, False))
        slots.append(row)
    return slots


def scatter_blocks(part, outer, inner):
    total = None
    for dz in range(outer - 1, -1, -1):
        row = None
        for dx in range(inner - 1, -1, -1):
            if row is None:
                row = part(dz, dx)
            else:
                moved = ring_shift(row.astype(BF16), -1, outer, inner, False)
                row = moved.astype(F32) + part(dz, dx)
        if total is None:
            total = row
        else:
            moved = ring_shift(total.astype(BF16), -1, outer, inner, True)
            total = moved.astype(F32) + row
    return total


def replica_shift(value, distance):
    count = lax.axis_size("replica")
    return lax.ppermute(
        value, "replica", [((i + distance) % count, i) for i in range(count)]
    )


def silu_slope(value):
    sigma = jax.nn.sigmoid(value)
    return sigma * (1.0 + value * (1.0 - sigma))


def dense_device(frames, cotangent, expert_ids, gate_weights, weight_in, weight_out):
    expert_count = lax.axis_size("expert")
    replica_count = lax.axis_size("replica")
    outer, inner = grid_of(expert_count)
    local_experts = weight_in.shape[1]
    all_experts = local_experts * expert_count
    frame_count = frames.shape[1]
    model_width = frames.shape[2]
    part_width = model_width // replica_count
    members = range(local_experts)
    others = range(1, replica_count)
    replica = lax.axis_index("replica")
    first_expert = lax.axis_index("expert") * local_experts

    with jax.named_scope("y_in"):
        parts_in = [weight_in[0]] + [replica_shift(weight_in[0], j) for j in others]

    def local_order(block):
        return jnp.roll(block, -replica * part_width, axis=1)

    gates = jnp.sum(
        jnp.where(
            expert_ids[0][:, :, None] == jnp.arange(all_experts, dtype=jnp.int32)[None, None, :],
            gate_weights[0][:, :, None],
            0.0,
        ),
        1,
    )
    high = lax.reduce_precision(gates, 8, 7)
    middle = lax.reduce_precision(gates - high, 8, 7)
    low = gates - high - middle
    gate_width = -(-3 * all_experts // 128) * 128
    gate_block = jnp.concatenate(
        [high, middle, low, jnp.zeros((frame_count, gate_width - 3 * all_experts), F32)], 1
    ).astype(BF16)
    lane = jnp.arange(gate_width, dtype=jnp.int32)[None, :]

    def gate_of(gate_rows, m):
        chosen = (lane < 3 * all_experts) & (lane % all_experts == first_expert + m)
        return jnp.sum(jnp.where(chosen, gate_rows.astype(F32), 0.0), 1, keepdims=True)

    def part_of(value, j):
        return value[:, j * part_width : (j + 1) * part_width]

    def gathered(block):
        slots = gather_blocks(block, outer, inner)
        return jnp.concatenate([b for row in slots for b in row], 0)

    own_x = local_order(frames[0])
    own_g = local_order(cotangent[0])
    with jax.named_scope("own"):
        rows = gathered(jnp.concatenate([own_x, own_g, gate_block], 1))
    rows_x = rows[:, :model_width]
    rows_g = rows[:, model_width : 2 * model_width]
    rows_gate = rows[:, 2 * model_width :]

    crossed = []
    for j in others:
        with jax.named_scope("y_cross"):
            block = jnp.concatenate(
                [
                    jnp.roll(own_x, j * part_width, axis=1),
                    part_of(own_g, replica_count - j),
                    gate_block,
                ],
                1,
            )
            crossed.append(replica_shift(block, j))

    parts_out = []
    for m in members:
        with jax.named_scope("y_out%d" % m):
            parts_out.append(
                [weight_out[0, m]] + [replica_shift(weight_out[0, m], j) for j in others]
            )

    with jax.named_scope("other"):
        other_rows = [gathered(block) for block in crossed]

    hidden = []
    slot_grads = []
    pre_list = []
    full_in = []
    for m in members:
        gate = gate_of(rows_gate, m)
        slot_grads.append((gate * rows_g.astype(F32)).astype(BF16))
        full_in.append(jnp.concatenate([p[m] for p in parts_in], 0))
        pre = jnp.dot(rows_x, full_in[m], preferred_element_type=F32)
        pre_list.append(pre)
        hidden.append(jax.nn.silu(pre).astype(BF16))

    def outer_sum(left, right):
        return lax.dot_general(
            left, right, (((0,), (0,)), ((), ())), preferred_element_type=F32
        )

    pre_grads = []
    in_sent = []
    for m in members:
        full_out = jnp.concatenate(parts_out[m], 1)
        hidden_grad = lax.dot_general(
            slot_grads[m], full_out, (((1,), (1,)), ((), ())), preferred_element_type=F32
        )
        pre_grads.append((hidden_grad * silu_slope(pre_list[m])).astype(BF16))
        with jax.named_scope("y_gin%d" % m):
            in_sent.append(
                [
                    replica_shift(outer_sum(part_of(rows_x, j), pre_grads[m]).astype(BF16), -j)
                    for j in others
                ]
            )

    row_grad = sum(
        lax.dot_general(
            pre_grads[m], full_in[m], (((1,), (1,)), ((), ())), preferred_element_type=F32
        )
        for m in members
    )

    def frame_part(dz, dx):
        start = (dz * inner + dx) * frame_count
        return row_grad[start : start + frame_count]

    with jax.named_scope("back"):
        total = scatter_blocks(frame_part, outer, inner)
    input_grad = jnp.roll(total.astype(BF16), replica * part_width, axis=1)[None]
    sections = lax.axis_size("section")
    sent_grads = lax.ppermute(
        input_grad, "section", [(i, (i + 1) % sections) for i in range(sections)]
    )

    grad_out = []
    for m in members:
        term = outer_sum(hidden[m], part_of(slot_grads[m], 0))
        for block in other_rows:
            pre = jnp.dot(block[:, :model_width], full_in[m], preferred_element_type=F32)
            gate = gate_of(block[:, model_width + part_width :], m)
            part = block[:, model_width : model_width + part_width].astype(F32)
            term = term + outer_sum(
                jax.nn.silu(pre).astype(BF16), (gate * part).astype(BF16)
            )
        grad_out.append(term.astype(BF16))

    grad_in = []
    for m in members:
        term = outer_sum(part_of(rows_x, 0), pre_grads[m])
        for received in in_sent[m]:
            term = term + received.astype(F32)
        grad_in.append(term.astype(BF16))
    return (sent_grads, jnp.stack(grad_in)[None], jnp.stack(grad_out)[None])


def shifted(block, axis, distance):
    devices = range(lax.axis_size(axis))
    route = [((i - distance) % len(devices), i) for i in devices]
    return lax.ppermute(block, axis, route)


def routed_device(frames, cotangent, expert_ids, gate_weights, weight_in, weight_out):
    expert_count = lax.axis_size("expert")
    local_experts = weight_in.shape[1]
    all_experts = local_experts * expert_count
    frame_count = frames.shape[1]
    model_width = frames.shape[2]
    choose_count = expert_ids.shape[2]
    capacity = max(frame_count * 3 // 16, frame_count * choose_count // all_experts)
    flat_ids = expert_ids[0].reshape(-1)
    flat_gate = gate_weights[0].reshape(-1)
    onehot = (flat_ids[:, None] == jnp.arange(all_experts, dtype=jnp.int32)[None, :]).astype(
        jnp.int32
    )
    position = jnp.sum((jnp.cumsum(onehot, 0) - 1) * onehot, 1)
    slot_index = flat_ids * capacity + position
    token_index = jnp.arange(frame_count * choose_count, dtype=jnp.int32) // choose_count
    rows_x = frames[0][token_index]
    rows_g = (flat_gate[:, None] * cotangent[0][token_index].astype(jnp.float32)).astype(
        jnp.bfloat16
    )
    empty = jnp.zeros((all_experts * capacity, model_width), jnp.bfloat16)
    send_x = (
        empty.at[slot_index].set(rows_x).reshape(expert_count, local_experts, capacity, model_width)
    )
    send_g = (
        empty.at[slot_index].set(rows_g).reshape(expert_count, local_experts, capacity, model_width)
    )
    recv_x, recv_g = (
        lax.all_to_all(send_x, "expert", split_axis=0, concat_axis=0, tiled=True),
        lax.all_to_all(send_g, "expert", split_axis=0, concat_axis=0, tiled=True),
    )
    full_in, full_out = (
        lax.all_gather(weight_in, "replica", axis=2, tiled=True),
        lax.all_gather(weight_out, "replica", axis=3, tiled=True),
    )
    row_count = expert_count * capacity
    hidden_list = []
    pregrad_list = []
    rowgrad_list = []
    for member in range(local_experts):
        inputs_x = recv_x[:, member].reshape(row_count, model_width)
        slot_grad = recv_g[:, member].reshape(row_count, model_width)
        w_first = full_in[0, member]
        w_second = full_out[0, member]
        pre = jnp.dot(inputs_x, w_first, preferred_element_type=jnp.float32)
        hidden = jax.nn.silu(pre).astype(jnp.bfloat16)
        hidden_grad = lax.dot_general(
            slot_grad, w_second, (((1,), (1,)), ((), ())), preferred_element_type=jnp.float32
        )
        pre_grad = (hidden_grad * silu_slope(pre)).astype(jnp.bfloat16)
        row_grad = lax.dot_general(
            pre_grad, w_first, (((1,), (1,)), ((), ())), preferred_element_type=jnp.float32
        )
        hidden_list.append(hidden)
        pregrad_list.append(pre_grad)
        rowgrad_list.append(
            row_grad.astype(jnp.bfloat16).reshape(expert_count, capacity, model_width)
        )
    returned = jnp.stack(rowgrad_list, 1)
    back = lax.all_to_all(returned, "expert", split_axis=0, concat_axis=0, tiled=True)
    back_rows = back.reshape(all_experts * capacity, model_width)[slot_index]
    summed = jnp.sum(
        back_rows.reshape(frame_count, choose_count, model_width).astype(jnp.float32), 1
    )
    sent_grads = shifted(summed.astype(jnp.bfloat16)[None], "section", 1)
    hidden_all = jnp.stack(hidden_list, 0)
    pregrad_all = jnp.stack(pregrad_list, 0)
    in_list = []
    out_list = []
    for member in range(local_experts):
        inputs_x = recv_x[:, member].reshape(row_count, model_width)
        slot_grad = recv_g[:, member].reshape(row_count, model_width)
        in_list.append(
            lax.dot_general(
                inputs_x,
                pregrad_all[member],
                (((0,), (0,)), ((), ())),
                preferred_element_type=jnp.float32,
            )
        )
        out_list.append(
            lax.dot_general(
                hidden_all[member],
                slot_grad,
                (((0,), (0,)), ((), ())),
                preferred_element_type=jnp.float32,
            )
        )
    terms_in = jnp.stack(in_list, 0)[None]
    terms_out = jnp.stack(out_list, 0)[None]
    summed_in, summed_out = (
        lax.psum_scatter(
            terms_in.astype(jnp.bfloat16), "replica", scatter_dimension=2, tiled=True
        ).astype(jnp.float32),
        lax.psum_scatter(
            terms_out.astype(jnp.bfloat16), "replica", scatter_dimension=3, tiled=True
        ).astype(jnp.float32),
    )
    grad_in = summed_in.astype(jnp.bfloat16)
    grad_out = summed_out.astype(jnp.bfloat16)
    return (sent_grads, grad_in, grad_out)


def per_device(frames, cotangent, expert_ids, gate_weights, weight_in, weight_out):
    frame_count = frames.shape[1]
    local_experts = weight_in.shape[1]
    all_experts = local_experts * lax.axis_size("expert")
    capacity = max(frame_count * 3 // 16, frame_count * expert_ids.shape[2] // all_experts)
    plan = dense_device if frame_count <= local_experts * capacity else routed_device
    return plan(frames, cotangent, expert_ids, gate_weights, weight_in, weight_out)


def solution(mesh):
    placed = (
        P("section", ("expert", "replica"), None),
        P("section", ("expert", "replica"), None),
        P("section", ("expert", "replica"), None),
        P("section", ("expert", "replica"), None),
        P("section", "expert", "replica", None),
        P("section", "expert", None, "replica"),
    )
    return jax.shard_map(
        per_device,
        mesh=mesh,
        in_specs=placed,
        out_specs=(
            P("section", ("expert", "replica"), None),
            P("section", "expert", "replica", None),
            P("section", "expert", None, "replica"),
        ),
        check_vma=False,
    )
```

```python
import jax
import jax.numpy as jnp
from jax import lax
from jax.sharding import PartitionSpec as P


F32 = jnp.float32
BF16 = jnp.bfloat16


def grid_of(count):
    inner = 1
    while inner * inner * 4 <= count and count % (inner * 2) == 0:
        inner *= 2
    return count // inner, inner


def ring_shift(value, distance, outer, inner, along_outer):
    route = []
    for i in range(outer * inner):
        z, x = divmod(i, inner)
        if along_outer:
            route.append((i, (z + distance) % outer * inner + x))
        else:
            route.append((i, z * inner + (x + distance) % inner))
    return lax.ppermute(value, "expert", route)


def after(value, *earlier):
    return lax.optimization_barrier((value,) + earlier)[0]


def gather_blocks(own, rounds, inner, gates=None, outer=None, done=()):
    outer = outer or rounds
    slots = list(done)
    column = slots[-1][0] if slots else own

    def step(value, dz, dx):
        gate = gates(dz, dx) if gates else ()
        return ring_shift(after(value, *gate) if gate else value, 1, outer, inner, dx == 0)

    for dz in range(len(slots), rounds):
        if dz:
            column = step(column, dz, 0)
        row = [column]
        for dx in range(1, inner):
            row.append(step(row[-1], dz, dx))
        slots.append(row)
    return slots


def scatter_blocks(part, outer, inner, marks):
    total = None
    for dz in range(outer - 1, -1, -1):
        row = None
        for dx in range(inner - 1, -1, -1):
            if row is None:
                row = part(dz, dx)
            else:
                moved = ring_shift(row.astype(BF16), -1, outer, inner, False)
                row = moved.astype(F32) + part(dz, dx)
        if total is not None:
            row = received.astype(F32) + row
        total = row
        if dz:
            marks.append(total.astype(BF16))
            received = ring_shift(marks[-1], -1, outer, inner, True)
    return total


def replica_shift(value, distance):
    count = lax.axis_size("replica")
    return lax.ppermute(
        value, "replica", [((i + distance) % count, i) for i in range(count)]
    )


def silu_slope(value):
    sigma = jax.nn.sigmoid(value)
    return sigma * (1.0 + value * (1.0 - sigma))


def dense_device(frames, cotangent, expert_ids, gate_weights, weight_in, weight_out):
    return dense_plan(frames, cotangent, expert_ids, gate_weights, weight_in, weight_out)


def dense_plan(frames, cotangent, expert_ids, gate_weights, weight_in, weight_out):
    expert_count = lax.axis_size("expert")
    replica_count = lax.axis_size("replica")
    outer, inner = grid_of(expert_count)
    local_experts = weight_in.shape[1]
    all_experts = local_experts * expert_count
    frame_count = frames.shape[1]
    model_width = frames.shape[2]
    part_width = model_width // replica_count
    members = range(local_experts)
    others = range(1, replica_count)
    replica = lax.axis_index("replica")
    first_expert = lax.axis_index("expert") * local_experts

    parts_in = [weight_in[0]] + [replica_shift(weight_in[0], j) for j in others]
    parts_out = []
    for m in members:
        parts_out.append([weight_out[0, m]] + [replica_shift(weight_out[0, m], j) for j in others])

    def local_order(block):
        return jnp.roll(block, -replica * part_width, axis=1)

    x_slots = gather_blocks(local_order(frames[0]), outer, inner)

    gates = jnp.sum(
        jnp.where(
            expert_ids[0][:, :, None] == jnp.arange(all_experts, dtype=jnp.int32)[None, None, :],
            gate_weights[0][:, :, None],
            0.0,
        ),
        1,
    )
    high = lax.reduce_precision(gates, 8, 7)
    middle = lax.reduce_precision(gates - high, 8, 7)
    low = gates - high - middle
    gate_width = -(-3 * all_experts // 128) * 128
    gate_block = jnp.concatenate(
        [high, middle, low, jnp.zeros((frame_count, gate_width - 3 * all_experts), F32)], 1
    ).astype(BF16)
    lane = jnp.arange(gate_width, dtype=jnp.int32)[None, :]
    g_slots = gather_blocks(
        jnp.concatenate([local_order(cotangent[0]), gate_block], 1), outer, inner
    )
    last_own = g_slots[-1][0]

    def gate_of(gate_rows, m):
        chosen = (lane < 3 * all_experts) & (lane % all_experts == first_expert + m)
        return jnp.sum(jnp.where(chosen, gate_rows.astype(F32), 0.0), 1, keepdims=True)

    def part_of(value, j):
        return value[:, j * part_width : (j + 1) * part_width]

    def joined(slots):
        return jnp.concatenate([after(b, last_own) for row in slots for b in row], 0)

    def outer_sum(left, right):
        return lax.dot_general(
            left, right, (((0,), (0,)), ((), ())), preferred_element_type=F32
        )

    rows_x = joined(x_slots)
    rows = joined(g_slots)
    rows_g = rows[:, :model_width]
    rows_gate = rows[:, model_width:]
    hidden = []
    slot_grads = []
    pre_list = []
    full_in = []
    out_sent = []
    out_terms = []
    for m in members:
        gate = gate_of(rows_gate, m)
        slot_grads.append((gate * rows_g.astype(F32)).astype(BF16))
        full_in.append(
            jnp.concatenate([parts_in[0][m]] + [after(p, last_own)[m] for p in parts_in[1:]], 0)
        )
        pre = jnp.dot(rows_x, full_in[m], preferred_element_type=F32)
        pre_list.append(pre)
        hidden.append(jax.nn.silu(pre).astype(BF16))
        terms = [outer_sum(hidden[m], part_of(slot_grads[m], j)).astype(BF16) for j in others]
        out_sent.append([replica_shift(t, -j) for j, t in zip(others, terms)])
        out_terms.extend(terms)

    pre_grads = []
    in_terms = []
    in_sent = []
    for m in members:
        full_out = jnp.concatenate(
            parts_out[m][:1] + [after(p, *out_terms) for p in parts_out[m][1:]], 1
        )
        hidden_grad = lax.dot_general(
            slot_grads[m], full_out, (((1,), (1,)), ((), ())), preferred_element_type=F32
        )
        pre_grads.append((hidden_grad * silu_slope(pre_list[m])).astype(BF16))

    row_grad = sum(
        lax.dot_general(
            pre_grads[m], full_in[m], (((1,), (1,)), ((), ())), preferred_element_type=F32
        )
        for m in members
    )
    for m in members:
        terms = [outer_sum(part_of(rows_x, j), pre_grads[m]).astype(BF16) for j in others]
        in_sent.append([replica_shift(t, -j) for j, t in zip(others, terms)])
        in_terms.extend(terms)

    def frame_part(dz, dx):
        start = (dz * inner + dx) * frame_count
        return row_grad[start : start + frame_count]

    marks = []
    total = scatter_blocks(frame_part, outer, inner, marks)
    input_grad = jnp.roll(total.astype(BF16), replica * part_width, axis=1)[None]
    sections = lax.axis_size("section")
    sent_grads = lax.ppermute(
        input_grad, "section", [(i, (i + 1) % sections) for i in range(sections)]
    )

    def summed(own, sent, *earlier):
        total = own
        for received in sent:
            total = total + (after(received, *earlier) if earlier else received).astype(F32)
        return total.astype(BF16)

    grad_out = [
        summed(
            outer_sum(after(hidden[m], *in_terms), part_of(slot_grads[m], 0)).astype(BF16).astype(F32),
            out_sent[m], *in_terms
        )
        for m in members
    ]
    grad_in = [
        summed(
            outer_sum(after(part_of(rows_x, 0), *in_terms), pre_grads[m]).astype(BF16).astype(F32),
            in_sent[m], input_grad
        )
        for m in members
    ]
    return (sent_grads, jnp.stack(grad_in)[None], jnp.stack(grad_out)[None])


def shifted(block, axis, distance):
    devices = range(lax.axis_size(axis))
    route = [((i - distance) % len(devices), i) for i in devices]
    return lax.ppermute(block, axis, route)


def routed_device(frames, cotangent, expert_ids, gate_weights, weight_in, weight_out):
    expert_count = lax.axis_size("expert")
    local_experts = weight_in.shape[1]
    all_experts = local_experts * expert_count
    frame_count = frames.shape[1]
    model_width = frames.shape[2]
    choose_count = expert_ids.shape[2]
    capacity = max(frame_count * 3 // 16, frame_count * choose_count // all_experts)
    flat_ids = expert_ids[0].reshape(-1)
    flat_gate = gate_weights[0].reshape(-1)
    onehot = (flat_ids[:, None] == jnp.arange(all_experts, dtype=jnp.int32)[None, :]).astype(
        jnp.int32
    )
    position = jnp.sum((jnp.cumsum(onehot, 0) - 1) * onehot, 1)
    slot_index = flat_ids * capacity + position
    token_index = jnp.arange(frame_count * choose_count, dtype=jnp.int32) // choose_count
    rows_x = frames[0][token_index]
    rows_g = (flat_gate[:, None] * cotangent[0][token_index].astype(jnp.float32)).astype(
        jnp.bfloat16
    )
    empty = jnp.zeros((all_experts * capacity, model_width), jnp.bfloat16)
    send_x = (
        empty.at[slot_index].set(rows_x).reshape(expert_count, local_experts, capacity, model_width)
    )
    send_g = (
        empty.at[slot_index].set(rows_g).reshape(expert_count, local_experts, capacity, model_width)
    )
    recv_x, recv_g = (
        lax.all_to_all(send_x, "expert", split_axis=0, concat_axis=0, tiled=True),
        lax.all_to_all(send_g, "expert", split_axis=0, concat_axis=0, tiled=True),
    )
    full_in, full_out = (
        lax.all_gather(weight_in, "replica", axis=2, tiled=True),
        lax.all_gather(weight_out, "replica", axis=3, tiled=True),
    )
    row_count = expert_count * capacity
    hidden_list = []
    pregrad_list = []
    rowgrad_list = []
    for member in range(local_experts):
        inputs_x = recv_x[:, member].reshape(row_count, model_width)
        slot_grad = recv_g[:, member].reshape(row_count, model_width)
        w_first = full_in[0, member]
        w_second = full_out[0, member]
        pre = jnp.dot(inputs_x, w_first, preferred_element_type=jnp.float32)
        hidden = jax.nn.silu(pre).astype(jnp.bfloat16)
        hidden_grad = lax.dot_general(
            slot_grad, w_second, (((1,), (1,)), ((), ())), preferred_element_type=jnp.float32
        )
        pre_grad = (hidden_grad * silu_slope(pre)).astype(jnp.bfloat16)
        row_grad = lax.dot_general(
            pre_grad, w_first, (((1,), (1,)), ((), ())), preferred_element_type=jnp.float32
        )
        hidden_list.append(hidden)
        pregrad_list.append(pre_grad)
        rowgrad_list.append(
            row_grad.astype(jnp.bfloat16).reshape(expert_count, capacity, model_width)
        )
    returned = jnp.stack(rowgrad_list, 1)
    back = lax.all_to_all(returned, "expert", split_axis=0, concat_axis=0, tiled=True)
    back_rows = back.reshape(all_experts * capacity, model_width)[slot_index]
    summed = jnp.sum(
        back_rows.reshape(frame_count, choose_count, model_width).astype(jnp.float32), 1
    )
    sent_grads = shifted(summed.astype(jnp.bfloat16)[None], "section", 1)
    hidden_all = jnp.stack(hidden_list, 0)
    pregrad_all = jnp.stack(pregrad_list, 0)
    in_list = []
    out_list = []
    for member in range(local_experts):
        inputs_x = recv_x[:, member].reshape(row_count, model_width)
        slot_grad = recv_g[:, member].reshape(row_count, model_width)
        in_list.append(
            lax.dot_general(
                inputs_x,
                pregrad_all[member],
                (((0,), (0,)), ((), ())),
                preferred_element_type=jnp.float32,
            )
        )
        out_list.append(
            lax.dot_general(
                hidden_all[member],
                slot_grad,
                (((0,), (0,)), ((), ())),
                preferred_element_type=jnp.float32,
            )
        )
    terms_in = jnp.stack(in_list, 0)[None]
    terms_out = jnp.stack(out_list, 0)[None]
    summed_in, summed_out = (
        lax.psum_scatter(
            terms_in.astype(jnp.bfloat16), "replica", scatter_dimension=2, tiled=True
        ).astype(jnp.float32),
        lax.psum_scatter(
            terms_out.astype(jnp.bfloat16), "replica", scatter_dimension=3, tiled=True
        ).astype(jnp.float32),
    )
    grad_in = summed_in.astype(jnp.bfloat16)
    grad_out = summed_out.astype(jnp.bfloat16)
    return (sent_grads, grad_in, grad_out)


def per_device(frames, cotangent, expert_ids, gate_weights, weight_in, weight_out):
    frame_count = frames.shape[1]
    local_experts = weight_in.shape[1]
    all_experts = local_experts * lax.axis_size("expert")
    capacity = max(frame_count * 3 // 16, frame_count * expert_ids.shape[2] // all_experts)
    plan = dense_device if frame_count <= local_experts * capacity else routed_device
    return plan(frames, cotangent, expert_ids, gate_weights, weight_in, weight_out)


def solution(mesh):
    placed = (
        P("section", ("expert", "replica"), None),
        P("section", ("expert", "replica"), None),
        P("section", ("expert", "replica"), None),
        P("section", ("expert", "replica"), None),
        P("section", "expert", "replica", None),
        P("section", "expert", None, "replica"),
    )
    return jax.shard_map(
        per_device,
        mesh=mesh,
        in_specs=placed,
        out_specs=(
            P("section", ("expert", "replica"), None),
            P("section", "expert", "replica", None),
            P("section", "expert", None, "replica"),
        ),
        check_vma=False,
    )
```
